128 devices in a mesh: sky: 16 (over z, x), src: 8 (over y, core).
Axes of the slice: x: 4, y: 4, z: 4, core: 2. Of those that a mesh axis runs over, the one named last changes fastest.
Arguments:
- exposures: float32 [16, 128, 256, 256], P('sky', 'src'), may hold values from -6 to 6
- variance: float32 [16, 128, 256, 256], P('sky', 'src'), may hold values from 0.25 to 4
- coef_table: float32 [64, 45], replicated, may hold values from -6 to 6
- coef_index: int32 [16, 128], P('sky', 'src'), may hold values from 0 to 63
- offsets: int32 [16, 128, 2], P('sky', 'src'), may hold values from 0 to 256
- tile_codes: int32 [16, 128], P('sky', 'src'), may hold values from 0 to 15, as said below
- detect_ra: float32 [41], replicated, may hold values from -1 to 1
- detect_dec: float32 [41], replicated, may hold values from -1 to 1
Outputs:
- coadd: float32 [8192, 4096], P('sky', 'src')
- detection: float32 [8192, 4096], P('sky', 'src')
The draws below stay inside these ranges and needn't reach their ends.
Inputs may be any that keep to these rules, and one draw needn't show every extreme that they name: `tile_codes`: code c sends a tile to the patch row c // 8 after the holder's own (wrapping around) and to owner c mod 8 along src. On one device at most 2 tiles name the same code; in every sky row one code is named by exactly 2 tiles on every device of that row.
All inputs are finite; a program needn't handle non-finite values.
Results may differ from the reference program's by a relative error of at most 0.0003.
Values sent between devices are 32-bit elements; how exact they have to be, the bound alone decides.
No kernel may reach another device: no remote copies, remote signals or barrier semaphores. Data moves between devices by JAX's collectives and lax.ppermute only.
A program may use at most 192 MiB of HBM per device.

```python
import math
import jax
import jax.numpy as jnp
from jax import lax

TILE = 256
PATCH = 512
TILES_DEV = 16
NBASIS = 45
KSIZE = 21
DSIZE = 41
RIM = 20
NCOEF = 64
OWNERS = 8
RA_PATCHES = 16


def draw_tile_codes(key, part):
    code_total = 2 * OWNERS
    key_hot, key_order, key_place = jax.random.split(key, 3)
    hottest = jax.random.randint(key_hot, (RA_PATCHES,), 0, code_total)
    entries = jnp.arange(2 * code_total, dtype=jnp.int32)
    raw_scores = jax.random.randint(key_order, (RA_PATCHES, OWNERS, 2 * code_total), 0, 1048576)
    scores = raw_scores * (2 * code_total) + entries[None, None, :]
    is_hot = (entries % code_total)[None, None, :] == hottest[:, None, None]
    scores = jnp.where(is_hot, entries[None, None, :] - 2 * code_total, scores)
    ordering = jnp.argsort(scores, axis=-1, stable=True)
    chosen = (ordering[..., :TILES_DEV] % code_total).astype(jnp.int32)
    place_scores = jax.random.randint(key_place, (RA_PATCHES, OWNERS, TILES_DEV), 0, 1048576) * TILES_DEV + jnp.arange(TILES_DEV, dtype=jnp.int32)[None, None, :]
    shuffle = jnp.argsort(place_scores, axis=-1, stable=True)
    chosen = jnp.take_along_axis(chosen, shuffle, axis=-1)
    return chosen.reshape(RA_PATCHES, OWNERS * TILES_DEV).astype(jnp.int32)


def place_ends(result, key, smallest, largest):
    longest = result.shape.index(max(result.shape))
    spots = []
    for shift in (0, 1):
        where = [jax.random.randint(jax.random.fold_in(key, axis), (), 0, length) for axis, length in enumerate(result.shape)]
        where[longest] = (where[longest] + shift) % result.shape[longest]
        spots.append(tuple(where))
    return result.at[spots[0]].set(smallest).at[spots[1]].set(largest)


def block_levels(own_key, shape, cuts, least, top_value):
    level = 1.0
    for dim, parts in cuts:
        steps = jax.random.uniform(jax.random.fold_in(jax.random.fold_in(own_key, 6), dim), (parts,), jnp.float32, least / len(cuts), top_value / len(cuts))
        level = level * jnp.repeat(jnp.exp(steps), shape[dim] // parts).reshape((-1,) + (1,) * (len(shape) - 1 - dim))
    return level


def scatter_about(own_key, shape, deviation, bound, shards=(), held_as=jnp.bfloat16):
    drawn = deviation * jax.random.normal(own_key, shape, jnp.float32)
    if shards:
        drawn = drawn * block_levels(own_key, shape, shards, -0.22, 0.18)
    return jnp.clip(drawn, -bound, bound).astype(held_as)


def setup_inputs(seed: int = 0) -> dict:
    key_of = jax.random.split(jax.random.key(seed), 9)
    return {
        "exposures": scatter_about(key_of[0], (RA_PATCHES, OWNERS * TILES_DEV, TILE, TILE), 1.0, 6.0, ((0, 16), (1, 8)), jnp.float32),
        "variance": jnp.clip(jnp.exp(math.log(4.0) - 2.7725887 * jax.random.uniform(key_of[1], (RA_PATCHES, OWNERS * TILES_DEV, TILE, TILE), jnp.float32) ** block_levels(key_of[1], (RA_PATCHES, OWNERS * TILES_DEV, TILE, TILE), ((0, 16), (1, 8)), -0.2, 0.2)), 0.25, 4.0),
        "coef_table": scatter_about(key_of[2], (NCOEF, NBASIS), 1.0, 6.0, (), jnp.float32),
        "coef_index": place_ends(jax.random.randint(key_of[3], (RA_PATCHES, OWNERS * TILES_DEV), 0, NCOEF), jax.random.fold_in(key_of[3], 1), 0, NCOEF - 1).astype(jnp.int32),
        "offsets": place_ends(jax.random.randint(key_of[4], (RA_PATCHES, OWNERS * TILES_DEV, 2), 0, PATCH - TILE + 1), jax.random.fold_in(key_of[4], 1), 0, PATCH - TILE).astype(jnp.int32),
        "tile_codes": draw_tile_codes(jax.random.fold_in(key_of[8], 71), 0),
        "detect_ra": scatter_about(key_of[6], (DSIZE,), DSIZE ** -0.5, 1.0, (), jnp.float32),
        "detect_dec": scatter_about(key_of[7], (DSIZE,), DSIZE ** -0.5, 1.0, (), jnp.float32),
    }


SPREADS = (0.75, 1.5, 3.0)


def basis_filters():
    radius = KSIZE // 2
    centred = jnp.arange(KSIZE, dtype=jnp.float32) - radius
    along_x = []
    along_y = []
    for spread in SPREADS:
        gaussian = jnp.exp(-(centred * centred) / (2.0 * spread * spread))
        scaled = centred / spread
        for power_x in range(5):
            for power_y in range(5 - power_x):
                filter_x = gaussian * scaled ** power_x
                filter_y = gaussian * scaled ** power_y
                along_x.append(filter_x / jnp.sum(jnp.abs(filter_x)))
                along_y.append(filter_y / jnp.sum(jnp.abs(filter_y)))
    return jnp.stack(along_y, 1), jnp.stack(along_x, 1)


def psf_kernel(coefs, along_y, along_x):
    return jnp.dot(along_y * coefs[None, :], along_x.T, precision=lax.Precision.HIGHEST, preferred_element_type=jnp.float32)


def match_fft(exposure, kernel):
    radius = KSIZE // 2
    extent = exposure.shape[0]
    full_len = extent + 2 * radius
    flipped = kernel[::-1, ::-1]
    spectrum = jnp.fft.rfft2(exposure, s=(full_len, full_len)) * jnp.fft.rfft2(flipped, s=(full_len, full_len))
    whole = jnp.fft.irfft2(spectrum, s=(full_len, full_len))
    return whole[radius:radius + extent, radius:radius + extent].astype(jnp.float32)


def reference(exposures, variance, coef_table, coef_index, offsets, tile_codes, detect_ra, detect_dec):
    along_y, along_x = basis_filters()
    per_row = exposures.shape[1]
    flat_tiles = exposures.reshape(-1, TILE, TILE)
    flat_var = variance.reshape(-1, TILE, TILE)
    flat_index = coef_index.reshape(-1).astype(jnp.int32)
    flat_offsets = offsets.reshape(-1, 2).astype(jnp.int32)
    flat_codes = tile_codes.reshape(-1).astype(jnp.int32)
    sky_rows = (jnp.arange(flat_codes.shape[0]) // per_row).astype(jnp.int32)

    def weighted_match(entry):
        exposure, var_tile, index_one = entry
        kernel = psf_kernel(coef_table[index_one], along_y, along_x)
        weight_map = 1.0 / var_tile
        return weight_map * match_fft(exposure, kernel), weight_map

    matched, weights = lax.map(weighted_match, (flat_tiles, flat_var, flat_index))

    def accumulate(totals, entry):
        numerator, denominator = totals
        matched_one, weight_one, corner, code_one, row_one = entry
        dest_row = ((row_one + code_one // OWNERS) % RA_PATCHES) * PATCH + corner[0]
        dest_col = (code_one % OWNERS) * PATCH + corner[1]
        anchor = (dest_row.astype(jnp.int32), dest_col.astype(jnp.int32))
        numerator = lax.dynamic_update_slice(numerator, lax.dynamic_slice(numerator, anchor, (TILE, TILE)) + matched_one, anchor)
        denominator = lax.dynamic_update_slice(denominator, lax.dynamic_slice(denominator, anchor, (TILE, TILE)) + weight_one, anchor)
        return (numerator, denominator), None

    blank = jnp.zeros((RA_PATCHES * PATCH, OWNERS * PATCH), jnp.float32)
    totals, ignored = lax.scan(accumulate, (blank, blank), (matched, weights, flat_offsets, flat_codes, sky_rows))
    numerator, denominator = totals
    coadd = numerator / (denominator + 1.0)
    grid_rows = coadd.shape[0]
    grid_cols = coadd.shape[1]
    col_padded = jnp.pad(coadd, ((0, 0), (RIM, RIM)))
    filtered = jnp.zeros_like(coadd)
    for tap_index in range(DSIZE):
        filtered = filtered + detect_dec[tap_index] * col_padded[:, tap_index:tap_index + grid_cols]
    wrapped = jnp.concatenate([filtered[grid_rows - RIM:], filtered, filtered[:RIM]], 0)
    detection = jnp.zeros_like(coadd)
    for tap_index in range(DSIZE):
        detection = detection + detect_ra[tap_index] * wrapped[tap_index:tap_index + grid_rows]
    return coadd, detection
```

```python
import functools

import jax
import jax.numpy as jnp
import numpy as np
from jax import lax
from jax.experimental import pallas as pl
from jax.experimental.pallas import tpu as pltpu
from jax.sharding import PartitionSpec as P

TILE = 256
PATCH = 512
KSIZE = 21
DSIZE = 41
RIM = 20
TILES = 16
SLOTS = 16
SPREADS = (0.75, 1.5, 3.0)
F32 = jnp.float32
BF16 = jnp.bfloat16


def basis_filters():
    u = np.arange(KSIZE, dtype=np.float32) - np.float32(KSIZE // 2)
    hx, hy = [], []
    for spread in SPREADS:
        g = np.exp(-(u * u) / np.float32(2.0 * spread * spread)).astype(np.float32)
        scaled = (u / np.float32(spread)).astype(np.float32)
        for p in range(5):
            for q in range(5 - p):
                fx = (g * scaled**p).astype(np.float32)
                fy = (g * scaled**q).astype(np.float32)
                hx.append(fx / np.sum(np.abs(fx)))
                hy.append(fy / np.sum(np.abs(fy)))
    return np.stack(hy, 1).astype(np.float32), np.stack(hx, 1).astype(np.float32)


def split(x):
    hi = x.astype(BF16)
    return hi, (x - hi.astype(F32)).astype(BF16)


def mm(a, b):
    return jnp.dot(a, b, preferred_element_type=F32)


def weights_body(info, codes, offs, v_ref, mine, part, dest, tab_mine, tab_part, buf, cnt, sem):
    n = pl.program_id(0)
    b = n & 1

    @pl.when(n == 0)
    def _():
        def zero(i, _):
            tab_mine[i] = 0
            tab_part[i] = 0
            return 0

        lax.fori_loop(0, 3 * SLOTS, zero, 0)

        def zero_count(i, _):
            cnt[i] = 0
            return 0

        lax.fori_loop(0, 16, zero_count, 0)

    code = codes[n]
    rank = cnt[code]
    cnt[code] = rank + 1
    owner = code & 7
    away = ((owner >> 1) - info[0]) & 3
    par = (owner & 1) ^ info[1]
    slot = (((code >> 3) * 4 + away) * 2) + rank
    dest[n] = par * SLOTS + slot

    @pl.when(n >= 2)
    def _():
        pltpu.make_async_copy(buf.at[b], mine.at[0], sem.at[b]).wait()

    buf[b] = 1.0 / v_ref[0]

    @pl.when(par == 0)
    def _():
        tab_mine[slot * 3] = 1
        tab_mine[slot * 3 + 1] = offs[2 * n]
        tab_mine[slot * 3 + 2] = offs[2 * n + 1]
        pltpu.make_async_copy(buf.at[b], mine.at[slot], sem.at[b]).start()

    @pl.when(par != 0)
    def _():
        tab_part[slot * 3] = 1
        tab_part[slot * 3 + 1] = offs[2 * n]
        tab_part[slot * 3 + 2] = offs[2 * n + 1]
        pltpu.make_async_copy(buf.at[b], part.at[slot], sem.at[b]).start()

    @pl.when(n == TILES - 1)
    def _():
        pltpu.make_async_copy(buf.at[1 - b], mine.at[0], sem.at[1 - b]).wait()
        pltpu.make_async_copy(buf.at[b], mine.at[0], sem.at[b]).wait()


def weights(info, codes, offs, variance):
    slots = jax.ShapeDtypeStruct((SLOTS, TILE, TILE), F32)
    table = jax.ShapeDtypeStruct((3 * SLOTS,), jnp.int32)
    return pl.pallas_call(
        weights_body,
        out_shape=(slots, slots, jax.ShapeDtypeStruct((TILES,), jnp.int32), table, table),
        grid_spec=pltpu.PrefetchScalarGridSpec(
            num_scalar_prefetch=3,
            grid=(TILES,),
            in_specs=[pl.BlockSpec((1, TILE, TILE), lambda n, *_: (n, 0, 0))],
            out_specs=(
                pl.BlockSpec(memory_space=pl.ANY),
                pl.BlockSpec(memory_space=pl.ANY),
                pl.BlockSpec(memory_space=pltpu.SMEM),
                pl.BlockSpec(memory_space=pltpu.SMEM),
                pl.BlockSpec(memory_space=pltpu.SMEM),
            ),
            scratch_shapes=[
                pltpu.VMEM((2, TILE, TILE), F32),
                pltpu.SMEM((16,), jnp.int32),
                pltpu.SemaphoreType.DMA((2,)),
            ],
        ),
        cost_estimate=pl.CostEstimate(flops=1 << 20, bytes_accessed=8 << 20, transcendentals=0),
        name="weights",
    )(info, codes, offs, variance)


def build_rows(g_ref, s, out):
    base = jnp.broadcast_to(g_ref[0, pl.ds(s, 1), :], (16, TILE))
    first = pltpu.roll(base, 0, 1, stride=1, stride_axis=0)
    row = lax.broadcasted_iota(jnp.int32, (16, TILE), 0)
    lane = lax.broadcasted_iota(jnp.int32, (16, TILE), 1)
    for i in range(8):
        band = first if i == 0 else pltpu.roll(first, 16 * i, 1)
        other = jnp.concatenate([band[:, 128:], band[:, :128]], axis=1)
        if i == 0:
            band = jnp.where(lane - row <= 10, band, 0.0)
        if i == 7:
            other = jnp.where(row + 240 - lane <= 10, other, 0.0)
        for at, rows in ((i, band), (i + 8, other)):
            hi, lo = split(rows)
            out[16 * at : 16 * at + 16, :] = hi
            out[TILE + 16 * at : TILE + 16 * at + 16, :] = lo


def match_body(dest, e_ref, v_ref, g_ref, mine, part, both, b0, b1, acc, buf, sem):
    n = pl.program_id(0)
    b = n & 1
    hi, lo = split(e_ref[0])
    both[0:TILE, :] = hi
    both[TILE : 2 * TILE, :] = lo
    acc[...] = jnp.zeros_like(acc)

    def add_rows(w, s):
        two = mm(both[...], w[0:TILE, :])
        sums = two[0:TILE] + two[TILE:] + mm(both[0:TILE, :], w[TILE : 2 * TILE, :])
        low = pl.multiple_of(16 - 8 * (s >> 3), 8)
        acc[s & 7, pl.ds(low, TILE), :] += sums

    build_rows(g_ref, 0, b0)

    def pair(i, _):
        s = 2 * i
        build_rows(g_ref, s + 1, b1)
        add_rows(b0, s)
        build_rows(g_ref, s + 2, b0)
        add_rows(b1, s + 1)
        return 0

    lax.fori_loop(0, 10, pair, 0)
    add_rows(b0, jnp.int32(20))

    matched = acc[0, 6 : 6 + TILE, :]
    for r in range(1, 8):
        matched = matched + acc[r, r + 6 : r + 6 + TILE, :]

    @pl.when(n >= 2)
    def _():
        pltpu.make_async_copy(buf.at[b], mine.at[0], sem.at[b]).wait()

    buf[b] = matched * (1.0 / v_ref[0])
    where = dest[n]

    @pl.when(where < SLOTS)
    def _():
        pltpu.make_async_copy(buf.at[b], mine.at[where], sem.at[b]).start()

    @pl.when(where >= SLOTS)
    def _():
        pltpu.make_async_copy(buf.at[b], part.at[where - SLOTS], sem.at[b]).start()

    @pl.when(n == TILES - 1)
    def _():
        pltpu.make_async_copy(buf.at[1 - b], mine.at[0], sem.at[1 - b]).wait()
        pltpu.make_async_copy(buf.at[b], mine.at[0], sem.at[b]).wait()


def match(dest, exposures, variance, rows):
    slots = jax.ShapeDtypeStruct((SLOTS, TILE, TILE), F32)
    tile = pl.BlockSpec((1, TILE, TILE), lambda n, *_: (n, 0, 0))
    return pl.pallas_call(
        match_body,
        out_shape=(slots, slots),
        grid_spec=pltpu.PrefetchScalarGridSpec(
            num_scalar_prefetch=1,
            grid=(TILES,),
            in_specs=[tile, tile, pl.BlockSpec((1, 24, TILE), lambda n, *_: (n, 0, 0))],
            out_specs=(pl.BlockSpec(memory_space=pl.ANY), pl.BlockSpec(memory_space=pl.ANY)),
            scratch_shapes=[
                pltpu.VMEM((2 * TILE, TILE), BF16),
                pltpu.VMEM((2 * TILE, TILE), BF16),
                pltpu.VMEM((2 * TILE, TILE), BF16),
                pltpu.VMEM((8, TILE + 16, TILE), F32),
                pltpu.VMEM((2, TILE, TILE), F32),
                pltpu.SemaphoreType.DMA((2,)),
            ],
        ),
        cost_estimate=pl.CostEstimate(
            flops=16 * 63 * 2 * 256**3, bytes_accessed=12 << 20, transcendentals=0
        ),
        name="match",
    )(dest, exposures, variance, rows)


def place(canvas, tile_ref, k, r, c):
    rq, rr, cq, cr = r >> 3, r & 7, c >> 7, c & 127
    columns = pl.ds(pl.multiple_of(cq * 128, 128), 384)
    keep_lane = lax.broadcasted_iota(jnp.int32, (64, 128), 1) >= cr
    keep_row = lax.broadcasted_iota(jnp.int32, (8, 8, 384), 1) >= rr
    carry = jnp.zeros((1, 8, 384), F32)
    for chunk in range(4):
        rows = slice(64 * chunk, 64 * chunk + 64)
        left = pltpu.roll(tile_ref[k, rows, 0:128], cr, 1)
        right = pltpu.roll(tile_ref[k, rows, 128:256], cr, 1)
        wide = jnp.concatenate(
            [
                jnp.where(keep_lane, left, 0.0),
                jnp.where(keep_lane, right, left),
                jnp.where(keep_lane, 0.0, right),
            ],
            axis=1,
        )
        turned = pltpu.roll(wide.reshape(8, 8, 384), rr, 1)
        above = jnp.concatenate([carry, turned[:7]], axis=0)
        canvas[pl.ds(rq + 8 * chunk, 8), :, columns] += jnp.where(keep_row, turned, above)
        carry = turned[7:8]
    canvas[pl.ds(rq + 32, 1), :, columns] += jnp.where(keep_row[0:1], 0.0, carry)


def gather_body(row, tab_mine, tab_other, mine, other, keep, plus, minus, hold, canvas):
    away = pl.program_id(0)
    canvas[...] = jnp.zeros_like(canvas)
    for table, ref in ((tab_mine, mine), (tab_other, other)):
        for k in range(2):
            at = ((row * 4 + away) * 2 + k) * 3

            @pl.when(table[at] == 1)
            def _():
                place(canvas, ref, k, table[at + 1], table[at + 2])

    def top():
        return canvas[0:32, :, 0:PATCH].reshape(TILE, PATCH)

    def bottom():
        return canvas[32:64, :, 0:PATCH].reshape(TILE, PATCH)

    @pl.when(away == 0)
    def _():
        keep[0] = top()
        keep[1] = bottom()

    @pl.when(away == 1)
    def _():
        hold[0] = top()
        plus[1] = bottom()

    @pl.when(away == 2)
    def _():
        plus[0] = top()
        minus[0] = bottom()

    @pl.when(away == 3)
    def _():
        minus[1] = top()
        hold[1] = bottom()


def gather(row, tab_mine, tab_other, mine, other):
    halves = jax.ShapeDtypeStruct((2, TILE, PATCH), F32)
    whole = pl.BlockSpec((2, TILE, PATCH), lambda d, *_: (0, 0, 0))
    pair = pl.BlockSpec((2, TILE, TILE), lambda d, *_: (row * 4 + d, 0, 0))
    return pl.pallas_call(
        functools.partial(gather_body, row),
        out_shape=(halves,) * 4,
        grid_spec=pltpu.PrefetchScalarGridSpec(
            num_scalar_prefetch=2,
            grid=(4,),
            in_specs=[pair, pair],
            out_specs=(whole,) * 4,
            scratch_shapes=[pltpu.VMEM((65, 8, 640), F32)],
        ),
        cost_estimate=pl.CostEstimate(flops=8 << 20, bytes_accessed=8 << 20, transcendentals=0),
        name="gather",
    )(tab_mine, tab_other, mine, other)


def taps_body(base_ref, out):
    base = jnp.broadcast_to(base_ref[0], (64, PATCH))
    first = pltpu.roll(base, 0, 1, stride=1, stride_axis=0)
    for i in range(8):
        band = first if i == 0 else pltpu.roll(first, 64 * i, 1)
        hi, lo = split(band)
        out[0, 0, 64 * i : 64 * i + 64, :] = hi
        out[0, 1, 64 * i : 64 * i + 64, :] = lo


def tap_matrices(bases):
    return pl.pallas_call(
        taps_body,
        out_shape=jax.ShapeDtypeStruct((2, 2, PATCH, PATCH), BF16),
        grid=(2,),
        in_specs=[pl.BlockSpec((1, 1, PATCH), lambda i: (i, 0, 0))],
        out_specs=pl.BlockSpec((1, 2, PATCH, PATCH), lambda i: (i, 0, 0, 0)),
        name="taps",
    )(bases)


def near(shape, row0, col0):
    row = lax.broadcasted_iota(jnp.int32, shape, 0) + row0
    col = lax.broadcasted_iota(jnp.int32, shape, 1) + col0
    return jnp.abs(row - col) <= RIM


def dot3(a_hi, a_lo, b_hi, b_lo):
    return mm(a_hi, b_hi) + mm(a_lo, b_hi) + mm(a_hi, b_lo)


def columns_body(c_ref, left, right, t_ref, out):
    inside = near((PATCH, PATCH), 0, 0)
    zero = jnp.zeros((), BF16)
    t_hi, t_lo = t_ref[0, 0], t_ref[0, 1]
    c_hi, c_lo = split(c_ref[...])
    out[...] = dot3(c_hi, c_lo, jnp.where(inside, t_hi, zero), jnp.where(inside, t_lo, zero))
    l_hi, l_lo = split(left[...])
    out[:, 0:128] += dot3(l_hi, l_lo, t_hi[384:, 0:128], t_lo[384:, 0:128])
    r_hi, r_lo = split(right[...])
    out[:, 384:] += dot3(r_hi, r_lo, t_hi[0:128, 384:], t_lo[0:128, 384:])


def rows_body(f_ref, above, below, t_ref, out, pad):
    inside = near((PATCH, PATCH), 0, 0)
    zero = jnp.zeros((), BF16)
    t_hi, t_lo = t_ref[0, 0], t_ref[0, 1]
    f_hi, f_lo = split(f_ref[...])
    out[...] = dot3(jnp.where(inside, t_hi, zero), jnp.where(inside, t_lo, zero), f_hi, f_lo)
    pad[...] = jnp.zeros_like(pad)
    pad[104:128, :] = above[...]
    a_hi, a_lo = split(pad[...])
    out[0:128, :] += dot3(t_hi[0:128, 384:], t_lo[0:128, 384:], a_hi, a_lo)
    pad[104:128, :] = jnp.zeros((24, PATCH), F32)
    pad[0:24, :] = below[...]
    b_hi, b_lo = split(pad[...])
    out[384:, :] += dot3(t_hi[384:, 0:128], t_lo[384:, 0:128], b_hi, b_lo)


def filter_columns(coadd, left, right, mats):
    return pl.pallas_call(
        columns_body,
        out_shape=jax.ShapeDtypeStruct((PATCH, PATCH), F32),
        grid=(1,),
        in_specs=[
            pl.BlockSpec((PATCH, PATCH), lambda i: (0, 0)),
            pl.BlockSpec((PATCH, 128), lambda i: (0, 0)),
            pl.BlockSpec((PATCH, 128), lambda i: (0, 0)),
            pl.BlockSpec((1, 2, PATCH, PATCH), lambda i: (0, 0, 0, 0)),
        ],
        out_specs=pl.BlockSpec((PATCH, PATCH), lambda i: (0, 0)),
        name="columns",
    )(coadd, left, right, mats)


def filter_rows(filtered, above, below, mats):
    return pl.pallas_call(
        rows_body,
        out_shape=jax.ShapeDtypeStruct((PATCH, PATCH), F32),
        grid=(1,),
        in_specs=[
            pl.BlockSpec((PATCH, PATCH), lambda i: (0, 0)),
            pl.BlockSpec((24, PATCH), lambda i: (0, 0)),
            pl.BlockSpec((24, PATCH), lambda i: (0, 0)),
            pl.BlockSpec((1, 2, PATCH, PATCH), lambda i: (1, 0, 0, 0)),
        ],
        out_specs=pl.BlockSpec((PATCH, PATCH), lambda i: (0, 0)),
        scratch_shapes=[pltpu.VMEM((128, PATCH), F32)],
        name="rows",
    )(filtered, above, below, mats)


def along(value, axis, steps, wrap=True):
    count = lax.axis_size(axis)
    pairs = [(i, (i + steps) % count) for i in range(count) if wrap or 0 <= i + steps < count]
    return lax.ppermute(value, axis, pairs)


def partner(value):
    return lax.ppermute(value, "src", [(i, i ^ 1) for i in range(lax.axis_size("src"))])


def reduce_ring(parts):
    keep, plus, minus, hold = parts
    got_plus = along(plus, "src", 2)
    got_minus = along(minus, "src", -2)
    on_plus = along(hold[0] + got_plus[0], "src", 2)
    on_minus = along(hold[1] + got_minus[0], "src", -2)
    top = keep[0] + on_plus + got_minus[1]
    bottom = keep[1] + got_plus[1] + on_minus
    return jnp.stack([top, bottom])


def on_device(
    exposures, variance, coef_table, coef_index, offsets, tile_codes, detect_ra, detect_dec
):
    me = lax.axis_index("src")
    info = jnp.stack([me >> 1, me & 1]).astype(jnp.int32)
    mine_w, part_w, dest, tab_mine, tab_part = weights(
        info, tile_codes[0], offsets[0].reshape(-1), variance[0]
    )
    tab_other = partner(tab_part)
    other_w = partner(part_w)

    along_y, along_x = basis_filters()
    turned = np.zeros((along_x.shape[1], TILE), np.float32)
    for lag in range(-10, 11):
        turned[:, lag % TILE] = along_x[10 - lag, :]
    picks = (coef_index[0][:, None] == jnp.arange(coef_table.shape[0])[None, :]).astype(F32)
    coefs = jnp.dot(picks, coef_table, precision=lax.Precision.HIGHEST)
    tall = np.concatenate([along_y, np.zeros((3, along_y.shape[1]), np.float32)])
    scaled = (jnp.asarray(tall)[None] * coefs[:, None, :]).reshape(TILES * 24, -1)
    rows = jnp.dot(scaled, jnp.asarray(turned), precision=lax.Precision.HIGHEST)
    rows = rows.reshape(TILES, 24, TILE)

    flip = detect_dec[::-1]
    gap = jnp.zeros((PATCH - DSIZE,), F32)
    bases = jnp.stack(
        [
            jnp.concatenate([flip[RIM:], gap, flip[:RIM]]),
            jnp.concatenate([detect_ra[RIM:], gap, detect_ra[:RIM]]),
        ]
    )[:, None, :]
    mats = tap_matrices(bases)

    den_next = gather(1, tab_mine, tab_other, mine_w, other_w)
    den_here = gather(0, tab_mine, tab_other, mine_w, other_w)
    mine_n, part_n = match(dest, exposures[0], variance[0], rows)
    other_n = partner(part_n)
    den1 = reduce_ring(den_next)
    den0 = reduce_ring(den_here)
    num_next = gather(1, tab_mine, tab_other, mine_n, other_n)
    num_here = gather(0, tab_mine, tab_other, mine_n, other_n)
    num1 = reduce_ring(num_next)
    num0 = reduce_ring(num_here)
    den = den0 + along(den1, "sky", 1)
    num = num0 + along(num1, "sky", 1)
    coadd = (num / (den + 1.0)).reshape(PATCH, PATCH)
    left = along(coadd[:, PATCH - 128 :], "src", 1, wrap=False)
    right = along(coadd[:, :128], "src", -1, wrap=False)
    filtered = filter_columns(coadd, left, right, mats)
    above = along(filtered[PATCH - 24 :], "sky", 1)
    below = along(filtered[:24], "sky", -1)
    detection = filter_rows(filtered, above, below, mats)
    return coadd, detection


def solution(mesh):
    return jax.shard_map(
        on_device,
        mesh=mesh,
        in_specs=(
            P("sky", "src", None, None),
            P("sky", "src", None, None),
            P(),
            P("sky", "src"),
            P("sky", "src", None),
            P("sky", "src"),
            P(),
            P(),
        ),
        out_specs=(P("sky", "src"), P("sky", "src")),
        check_vma=False,
    )
```
